32 devices in a mesh: ctx: 8 (over z, y), head: 4 (over x, core).
Axes of the slice: x: 2, y: 2, z: 4, core: 2. Of those that a mesh axis runs over, the one named last changes fastest.
Arguments:
- queries: bfloat16 [1024, 64, 128], P('ctx', 'head'), may hold values from -90 to 90
- key_states: bfloat16 [1024, 8, 128], P('ctx', 'head'), may hold values from -4.5 to 4.5
- value_states: bfloat16 [1024, 8, 128], P('ctx', 'head'), may hold values from -6 to 6
- chosen: int32 [2, 4], replicated, may hold values from 0 to 1, as said below
- valid_count: int32 [2], replicated, may hold values from 1 to 2, as said below
Outputs:
- attn_out: bfloat16 [1024, 64, 128], P('ctx', 'head')
- key_mass: float32 [64, 1024], P('head', 'ctx')
The draws below stay inside these ranges and needn't reach their ends.
Inputs may be any that keep to these rules, and one draw needn't show every extreme that they name: `chosen`: row i lists block i first; if valid_count[i] >= 2, block 0 second; the next valid_count[i] - 2 entries are distinct blocks from 1 to i - 1; entries from position valid_count[i] on equal i. valid_count[i] is at most min(4, i + 1), and the last block's count is min(4, 2).
All inputs are finite; a program needn't handle non-finite values.
Results may differ from the reference program's by a relative error of at most 0.0046.
Values may be sent and summed in bfloat16 or wider, within the bound.
A program may use at most 64 MiB of HBM per device.

```python
import math
import jax
import jax.numpy as jnp
from jax import lax

HEADS = 64
KV_HEADS = 8
HDIM = 128
BLOCK = 512
TOPK = 4
SEQ = 1024
NB = 2


def index_tables(key):
    base_key = jax.random.fold_in(key, 7)
    rank_key, want_key = jax.random.split(base_key)
    blocks = jnp.arange(NB, dtype=jnp.int32)
    rank_values = jax.random.randint(rank_key, (NB, NB), 0, 65536, dtype=jnp.int32) * NB + blocks[None, :]
    allowed = (blocks[None, :] >= 1) & (blocks[None, :] < blocks[:, None])
    sort_keys = jnp.where(allowed, rank_values, 65536 * NB + blocks[None, :])
    ordering = jnp.argsort(sort_keys, axis=1).astype(jnp.int32)
    pad_width = max(0, TOPK - 2 - NB)
    ordering = jnp.pad(ordering, ((0, 0), (0, pad_width)))[:, :TOPK - 2]
    listed = jnp.concatenate([blocks[:, None], jnp.zeros((NB, 1), jnp.int32), ordering], axis=1)
    wanted_count = jax.random.randint(want_key, (NB,), 1, TOPK + 1, dtype=jnp.int32)
    wanted_count = wanted_count.at[NB - 1].set(TOPK)
    counts = jnp.minimum(wanted_count, blocks + 1)
    slot_ids = jnp.arange(TOPK, dtype=jnp.int32)
    chosen_table = jnp.where(slot_ids[None, :] < counts[:, None], listed, blocks[:, None])
    return (chosen_table, counts)


def draw_chosen(key, part):
    return index_tables(key)[0]


def draw_valid_count(key, part):
    return index_tables(key)[1]


def drawn_states(key):
    base_key = jax.random.fold_in(key, 11)
    key_draw, query_draw = jax.random.split(base_key, 2)
    key_values = jnp.clip(jax.random.normal(key_draw, (SEQ, KV_HEADS, HDIM), jnp.float32), -4.5, 4.5)
    query_values = jnp.clip(jax.random.normal(query_draw, (SEQ, HEADS, HDIM), jnp.float32), -4.5, 4.5)
    return (query_values, key_values)


def draw_queries(key, part):
    return drawn_states(key)[0].astype(jnp.bfloat16)


def draw_key_states(key, part):
    return drawn_states(key)[1].astype(jnp.bfloat16)


def steps_of(stream_key, dims, cuts, least, high):
    def one(dim, shards_of):
        heights = jax.random.uniform(jax.random.fold_in(jax.random.fold_in(stream_key, 6), dim), (shards_of,), jnp.float32, least / len(cuts), high / len(cuts))
        return jnp.repeat(jnp.exp(heights), dims[dim] // shards_of).reshape((-1,) + (1,) * (len(dims) - dim - 1))

    level = one(*cuts[0])
    for cut in cuts[1:]:
        level = level * one(*cut)
    return level


def normal_values(stream_key, dims, width, most, pieces=(), held_as=jnp.bfloat16):
    factor_of = steps_of(stream_key, dims, pieces, -0.22, 0.18) if pieces else 1.0
    entries = jax.random.normal(stream_key, dims, jnp.float32) * width * factor_of
    return jnp.minimum(jnp.maximum(entries, -most), most).astype(held_as)


def setup_inputs(seed: int = 0) -> dict:
    arg_keys = jax.random.split(jax.random.key(seed), 6)
    queries = draw_queries(jax.random.fold_in(arg_keys[5], 71), 0)
    key_states = draw_key_states(jax.random.fold_in(arg_keys[5], 71), 0)
    value_states = normal_values(arg_keys[2], (SEQ, KV_HEADS, HDIM), 1.0, 6.0, ((0, 8), (1, 4)))
    chosen = draw_chosen(jax.random.fold_in(arg_keys[5], 71), 0)
    valid_count = draw_valid_count(jax.random.fold_in(arg_keys[5], 71), 0)
    return {"queries": queries, "key_states": key_states, "value_states": value_states, "chosen": chosen, "valid_count": valid_count}


def reference(queries, key_states, value_states, chosen, valid_count):
    groups = HEADS // KV_HEADS
    score_scale = 1.0 / math.sqrt(HDIM)
    key_blocks = key_states.reshape(NB, BLOCK, KV_HEADS, HDIM)
    value_blocks = value_states.reshape(NB, BLOCK, KV_HEADS, HDIM)
    query_blocks = queries.reshape(NB, BLOCK, KV_HEADS, groups, HDIM)
    offsets = jnp.arange(BLOCK, dtype=jnp.int32)
    slot_ids = jnp.arange(TOPK, dtype=jnp.int32)

    def one_block(attribution, block_index):
        listed = chosen[block_index]
        slot_valid = slot_ids < valid_count[block_index]
        key_tile = key_blocks[listed].reshape(TOPK * BLOCK, KV_HEADS, HDIM)
        value_tile = value_blocks[listed].reshape(TOPK * BLOCK, KV_HEADS, HDIM)
        key_pos = (listed[:, None] * BLOCK + offsets[None, :]).reshape(-1)
        key_block = jnp.repeat(listed, BLOCK)
        key_valid = jnp.repeat(slot_valid, BLOCK)
        query_pos = block_index * BLOCK + offsets
        visible = key_valid[None, :] & ((key_block[None, :] < block_index) | (key_pos[None, :] <= query_pos[:, None]))
        query_heads = jnp.transpose(query_blocks[block_index], (1, 2, 0, 3)).astype(jnp.float32)
        key_heads = jnp.transpose(key_tile, (1, 0, 2)).astype(jnp.float32)
        value_heads = jnp.transpose(value_tile, (1, 0, 2)).astype(jnp.float32)

        def per_head(items):
            query_one, key_one, value_one = items
            scores = jnp.einsum('gtd,ud->gtu', query_one, key_one) * score_scale
            scores = jnp.where(visible[None], scores, -jnp.inf)
            highest = lax.optimization_barrier(jnp.max(scores, axis=-1, keepdims=True))
            raised = jnp.exp(scores - highest)
            attention = raised / lax.optimization_barrier(jnp.sum(raised, axis=-1, keepdims=True))
            weights = attention.astype(jnp.bfloat16).astype(jnp.float32)
            mixed = jnp.einsum('gtu,ud->gtd', weights, value_one)
            return (mixed, lax.optimization_barrier(jnp.sum(attention, axis=1)))
        head_outputs, head_masses = lax.map(per_head, (query_heads, key_heads, value_heads))
        mixed = jnp.transpose(head_outputs, (2, 0, 1, 3)).reshape(BLOCK, HEADS, HDIM).astype(jnp.bfloat16)
        head_masses = head_masses.reshape(HEADS, TOPK, BLOCK)
        attribution = attribution.at[:, listed].add(head_masses)
        return (attribution, mixed)
    start_mass = jnp.zeros((HEADS, NB, BLOCK), jnp.float32)
    attribution, mixed_blocks = lax.scan(one_block, start_mass, jnp.arange(NB, dtype=jnp.int32))
    return (mixed_blocks.reshape(SEQ, HEADS, HDIM), attribution.reshape(HEADS, SEQ))
```

```python
import functools
import math

import jax
import jax.numpy as jnp
from jax import lax
from jax.experimental import pallas as pl
from jax.experimental.pallas import tpu as pltpu
from jax.sharding import PartitionSpec as P

BLOCK = 512
HIDDEN = -1e30
SEGMENTS = 4


def from_partner(value, axis, bit):
    mask = 2**bit
    pairs = [(source, source ^ mask) for source in range(lax.axis_size(axis))]
    return lax.ppermute(value, axis, pairs)


def on_device(queries, key_states, value_states, chosen, valid_count):
    ctx_size = lax.axis_size("ctx")
    my_index = lax.axis_index("ctx")
    token_count = queries.shape[0]
    query_heads = queries.shape[1]
    head_depth = queries.shape[2]
    kv_total = key_states.shape[1]
    groups = query_heads // kv_total
    slot_total = chosen.shape[1]
    split_count = BLOCK // token_count
    quarter = token_count // split_count
    my_block = my_index // split_count
    my_member = my_index % split_count
    listed = chosen[my_block]
    slot_ids = jnp.arange(slot_total)
    slot_valid = slot_ids < valid_count[my_block]
    owners = jnp.arange(ctx_size) // split_count
    wanted = jnp.any(
        (slot_ids[None, :] < valid_count[owners][:, None]) & (chosen[owners] == my_block), axis=1
    )
    stacked = jnp.stack([key_states, value_states]).reshape(
        2, 1, split_count, quarter, kv_total, head_depth
    )
    outgoing = jnp.broadcast_to(
        stacked, (2, ctx_size // split_count, split_count, quarter, kv_total, head_depth)
    )
    outgoing = outgoing.reshape(2, ctx_size, quarter, kv_total, head_depth)
    outgoing = jnp.where(wanted[None, :, None, None, None], outgoing, jnp.zeros((), outgoing.dtype))
    incoming = lax.all_to_all(outgoing, "ctx", split_axis=1, concat_axis=1, tiled=True)
    sources = (listed[:, None] * split_count + jnp.arange(split_count)[None, :]).reshape(-1)
    fetched = jnp.take(incoming, sources, axis=1)
    bit_total = split_count.bit_length() - 1
    for bit_index in range(bit_total):
        partner = from_partner(fetched, "ctx", bit_index)
        is_lower = my_member // 2**bit_index % 2 == 0
        fetched = jnp.where(
            is_lower,
            jnp.concatenate([fetched, partner], axis=2),
            jnp.concatenate([partner, fetched], axis=2),
        )
    fetched = fetched.reshape(2, slot_total * BLOCK, kv_total, head_depth)
    by_head = jnp.transpose(fetched, (0, 2, 1, 3))
    query_pos = my_index * token_count + jnp.arange(token_count)
    score_scale = 1.0 / math.sqrt(head_depth)
    grouped = queries.reshape(token_count, kv_total, groups, head_depth)
    offsets = jnp.arange(BLOCK)
    key_pos = (listed[:, None] * BLOCK + offsets[None, :]).reshape(-1)
    key_block = jnp.repeat(listed, BLOCK)
    key_valid = jnp.repeat(slot_valid, BLOCK)
    visibility = key_valid[None, :] & (
        (key_block[None, :] < my_block) | (key_pos[None, :] <= query_pos[:, None])
    )
    contract_last = (((1,), (1,)), ((), ()))
    head_outputs = []
    head_masses = []
    for kv_head in range(kv_total):
        key_head = by_head[0, kv_head]
        value_head = by_head[1, kv_head]
        for group_index in range(groups):
            raw_scores = (
                lax.dot_general(
                    grouped[:, kv_head, group_index],
                    key_head,
                    contract_last,
                    preferred_element_type=jnp.float32,
                )
                * score_scale
            )
            scores = jnp.where(visibility, raw_scores, -jnp.inf)
            highest = jnp.max(scores, axis=-1, keepdims=True)
            raised = jnp.exp(scores - highest)
            attention = raised / jnp.sum(raised, axis=-1, keepdims=True)
            head_outputs.append(
                jnp.dot(
                    attention.astype(jnp.bfloat16), value_head, preferred_element_type=jnp.float32
                )
            )
            head_masses.append(jnp.sum(attention, axis=0).reshape(slot_total, BLOCK))
    attn_out = jnp.stack(head_outputs, axis=1).astype(jnp.bfloat16)
    contrib = jnp.stack(head_masses, axis=1).reshape(
        slot_total, query_heads, split_count, token_count
    )
    contrib = jnp.transpose(contrib, (0, 2, 1, 3)).reshape(
        slot_total * split_count, query_heads, token_count
    )
    landing = jnp.zeros((ctx_size, query_heads, token_count), jnp.float32).at[sources].add(contrib)
    key_mass = lax.psum_scatter(landing, "ctx", scatter_dimension=0, tiled=True).reshape(
        query_heads, token_count
    )
    return (attn_out, key_mass)


def causal_kernel(
    n, q_hbm, k_hbm, v_hbm, out_ref, mass_ref,
    q_in, k_in, v_in, wide, q_all, k_all, v_all, scores, top, probs, mixed, mass, landed,
    in_sem, k_line, k_pair, k_recv, v_line, v_pair, v_recv, m_send, m_recv,
):
    me = lax.axis_index("ctx")
    level = me // 2
    side = me % 2
    levels = n // 2
    tokens, heads, depth = q_in.shape
    kv_total = heads // 8
    rows = tokens * 8
    partner = level * 2 + 1 - side
    above = lax.rem(me + 2, n)
    log2_scale = math.log2(math.e) / math.sqrt(depth)

    copies_in = [
        pltpu.make_async_copy(src, dst, in_sem.at[i])
        for i, (src, dst) in enumerate(((k_hbm, k_in), (v_hbm, v_in), (q_hbm, q_in)))
    ]
    for copy in copies_in:
        copy.start()
    barrier = pltpu.get_barrier_semaphore()
    for hop in range(1, n):
        pl.semaphore_signal(
            barrier, inc=1, device_id={"ctx": lax.rem(me + hop, n)},
            device_id_type=pl.DeviceIdType.MESH,
        )

    def split_heads(source, target):
        wide[...] = source[...].astype(jnp.float32)
        for kv in range(kv_total):
            target[me, kv] = wide[pl.ds(kv, tokens, stride=kv_total), :].astype(jnp.bfloat16)

    def remote(ref, slot, send_sem, recv_sem, target):
        return pltpu.make_async_remote_copy(
            src_ref=ref.at[slot], dst_ref=ref.at[slot],
            send_sem=send_sem.at[slot], recv_sem=recv_sem.at[slot],
            device_id={"ctx": target}, device_id_type=pl.DeviceIdType.MESH,
        )

    def line_slot(back):
        return (level - back) * 2 + side

    def pair_slot(back):
        return (level - back) * 2 + 1 - side

    def has_line(back):
        return level >= back

    def has_pair(back):
        return (level >= back) & (side == 1) if back == 0 else level >= back

    def sends(ref, back, line_sem, pair_sem, recv_sem, act):
        slot = line_slot(back)

        @pl.when((level >= back) & (level < levels - 1))
        def _():
            act(remote(ref, slot, line_sem, recv_sem, above))

        gives = (level >= back) & (side == 0) if back == 0 else level >= back

        @pl.when(gives)
        def _():
            act(remote(ref, slot, pair_sem, recv_sem, partner))

    def send_k(back, act):
        sends(k_all, back, k_line, k_pair, k_recv, act)

    def send_v(back, act):
        sends(v_all, back, v_line, v_pair, v_recv, act)

    def start(copy):
        copy.start()

    def arrive(ref, slot, send_sem, recv_sem):
        remote(ref, slot, send_sem, recv_sem, partner).wait_recv()

    def forward_k(back):
        @pl.when(has_line(back))
        def _():
            arrive(k_all, line_slot(back), k_line, k_recv)

        send_k(back, start)

    def forward_v(back):
        @pl.when(has_line(back))
        def _():
            arrive(v_all, line_slot(back), v_line, v_recv)

        send_v(back, start)

    def score(slot, own):
        for kv in range(kv_total):
            raw = lax.dot_general(
                q_all[kv], k_all[slot, kv], (((1,), (1,)), ((), ())),
                preferred_element_type=jnp.float32,
            )
            if own:
                raw = raw.reshape(tokens, 8, tokens)
                token = lax.broadcasted_iota(jnp.int32, raw.shape, 0)
                key = lax.broadcasted_iota(jnp.int32, raw.shape, 2)
                raw = jnp.where(key <= token, raw, HIDDEN).reshape(rows, tokens)
                top[kv] = raw
            else:
                top[kv] = jnp.maximum(top[kv], raw)
            scores[slot, kv] = raw

    def score_line(back):
        @pl.when(has_line(back))
        def _():
            score(line_slot(back), False)

    def score_pair(back):
        @pl.when(has_pair(back))
        def _():
            slot = pair_slot(back)
            arrive(k_all, slot, k_pair, k_recv)
            score(slot, False)

    copies_in[0].wait()
    split_heads(k_in, k_all)
    pl.semaphore_wait(barrier, n - 1)
    send_k(0, start)
    copies_in[1].wait()
    split_heads(v_in, v_all)
    copies_in[2].wait()
    for kv in range(kv_total):
        q_part = q_in[...].astype(jnp.float32)[:, kv * 8 : kv * 8 + 8, :]
        q_all[kv] = q_part.reshape(rows, depth).astype(jnp.bfloat16)
    score(me, True)
    for slot in range(1, n):

        @pl.when(slot > me)
        def _():
            scores[slot] = jnp.full(scores.shape[1:], HIDDEN, jnp.float32)

    for back in range(1, levels):
        forward_k(back)
        if back == 1:
            send_v(0, start)
        score_line(back)
        score_pair(back - 1)
    score_pair(levels - 1)

    mass[...] = jnp.zeros_like(mass)
    part_rows = 128
    parts = rows // part_rows
    total = kv_total * parts

    def soften(index, carry):
        kv = index // parts
        at = pl.ds(pl.multiple_of((index % parts) * part_rows, part_rows), part_rows)
        highest = jnp.max(top[kv, at, :], axis=-1, keepdims=True) * log2_scale
        summed = jnp.zeros((part_rows, tokens), jnp.float32)
        for slot in range(n):
            raised = jnp.exp2(scores[slot, kv, at, :] * log2_scale - highest)
            scores[slot, kv, at, :] = raised
            summed = summed + raised
        inverse = 1.0 / jnp.sum(summed, axis=-1, keepdims=True)
        for slot in range(n):
            attention = scores[slot, kv, at, :] * inverse
            probs[slot, kv, at, :] = attention.astype(jnp.bfloat16)
            mass[slot, kv] += jnp.sum(attention.reshape(part_rows // 8, 8, tokens), axis=0)
        return carry

    for segment in range(SEGMENTS):
        if 1 + segment < levels:
            forward_v(1 + segment)
        lax.fori_loop(segment * total // SEGMENTS, (segment + 1) * total // SEGMENTS, soften, 0)

    def mass_copy(source, target):
        return pltpu.make_async_remote_copy(
            src_ref=mass.at[target], dst_ref=landed.at[source],
            send_sem=m_send.at[target], recv_sem=m_recv.at[source],
            device_id={"ctx": target}, device_id_type=pl.DeviceIdType.MESH,
        )

    for slot in range(n - 1):

        @pl.when(slot < me)
        def _():
            mass_copy(me, slot).start()

    def mix(slot, first):
        for kv in range(kv_total):
            piece = jnp.dot(probs[slot, kv], v_all[slot, kv], preferred_element_type=jnp.float32)
            mixed[kv] = piece if first else mixed[kv] + piece

    def mix_line(back):
        @pl.when(has_line(back))
        def _():
            mix(line_slot(back), False)

    def mix_pair(back):
        @pl.when(has_pair(back))
        def _():
            slot = pair_slot(back)
            arrive(v_all, slot, v_pair, v_recv)
            mix(slot, False)

    mix(me, True)
    for back in range(1, levels):
        mix_line(back)
        mix_pair(back - 1)
    mix_pair(levels - 1)
    out_ref[...] = jnp.concatenate(
        [mixed[kv].reshape(tokens, 8, depth) for kv in range(kv_total)], axis=1
    ).astype(out_ref.dtype)

    mass_ref[...] = jnp.concatenate([mass[me, kv] for kv in range(kv_total)], axis=0)
    for slot in range(1, n):

        @pl.when(slot > me)
        def _():
            mass_copy(slot, me * 0 + partner).wait_recv()
            mass_ref[...] += jnp.concatenate([landed[slot, kv] for kv in range(kv_total)], axis=0)

    def wait_send(copy):
        copy.wait_send()

    for back in range(levels):
        send_k(back, wait_send)
        send_v(back, wait_send)
    for slot in range(n - 1):

        @pl.when(slot < me)
        def _():
            mass_copy(me, slot).wait_send()


def causal_step(n, queries, key_states, value_states):
    tokens, heads, depth = queries.shape
    kv_total = key_states.shape[1]
    rows = tokens * 8
    f32, bf16 = jnp.float32, jnp.bfloat16
    dma = pltpu.SemaphoreType.DMA
    return pl.pallas_call(
        functools.partial(causal_kernel, n),
        out_shape=(
            jax.ShapeDtypeStruct((tokens, heads, depth), bf16),
            jax.ShapeDtypeStruct((heads, tokens), f32),
        ),
        in_specs=[pl.BlockSpec(memory_space=pl.ANY)] * 3,
        out_specs=[pl.BlockSpec(memory_space=pltpu.VMEM)] * 2,
        scratch_shapes=[
            pltpu.VMEM((tokens, heads, depth), bf16),
            pltpu.VMEM((tokens * kv_total, depth), bf16),
            pltpu.VMEM((tokens * kv_total, depth), bf16),
            pltpu.VMEM((tokens * kv_total, depth), f32),
            pltpu.VMEM((kv_total, rows, depth), bf16),
            pltpu.VMEM((n, kv_total, tokens, depth), bf16),
            pltpu.VMEM((n, kv_total, tokens, depth), bf16),
            pltpu.VMEM((n, kv_total, rows, tokens), f32),
            pltpu.VMEM((kv_total, rows, tokens), f32),
            pltpu.VMEM((n, kv_total, rows, tokens), bf16),
            pltpu.VMEM((kv_total, rows, depth), f32),
            pltpu.VMEM((n, kv_total, 8, tokens), f32),
            pltpu.VMEM((n, kv_total, 8, tokens), f32),
            dma((3,)), dma((n,)), dma((n,)), dma((n,)), dma((n,)), dma((n,)), dma((n,)),
            dma((n,)), dma((n,)),
        ],
        compiler_params=pltpu.CompilerParams(
            collective_id=0, has_side_effects=True, vmem_limit_bytes=40 * 1024 * 1024
        ),
    )(
        queries,
        key_states.reshape(tokens * kv_total, depth),
        value_states.reshape(tokens * kv_total, depth),
    )


def solution(mesh):
    in_specs = (P("ctx", "head", None), P("ctx", "head", None), P("ctx", "head", None), P(), P())
    out_specs = (P("ctx", "head", None), P("head", "ctx"))

    def step(queries, key_states, value_states, chosen, valid_count):
        if chosen.shape[0] <= 2 and mesh.shape["ctx"] % 2 == 0:
            return causal_step(mesh.shape["ctx"], queries, key_states, value_states)
        return on_device(queries, key_states, value_states, chosen, valid_count)

    return jax.shard_map(step, mesh=mesh, in_specs=in_specs, out_specs=out_specs, check_vma=False)
```

```python
import functools
import math

import jax
import jax.numpy as jnp
from jax import lax
from jax.experimental import pallas as pl
from jax.experimental.pallas import tpu as pltpu
from jax.sharding import PartitionSpec as P

BLOCK = 512
HIDDEN = -1e30
SEGMENTS = 4


def from_partner(value, axis, bit):
    mask = 2**bit
    pairs = [(source, source ^ mask) for source in range(lax.axis_size(axis))]
    return lax.ppermute(value, axis, pairs)


def on_device(queries, key_states, value_states, chosen, valid_count):
    ctx_size = lax.axis_size("ctx")
    my_index = lax.axis_index("ctx")
    token_count = queries.shape[0]
    query_heads = queries.shape[1]
    head_depth = queries.shape[2]
    kv_total = key_states.shape[1]
    groups = query_heads // kv_total
    slot_total = chosen.shape[1]
    split_count = BLOCK // token_count
    quarter = token_count // split_count
    my_block = my_index // split_count
    my_member = my_index % split_count
    listed = chosen[my_block]
    slot_ids = jnp.arange(slot_total)
    slot_valid = slot_ids < valid_count[my_block]
    owners = jnp.arange(ctx_size) // split_count
    wanted = jnp.any(
        (slot_ids[None, :] < valid_count[owners][:, None]) & (chosen[owners] == my_block), axis=1
    )
    stacked = jnp.stack([key_states, value_states]).reshape(
        2, 1, split_count, quarter, kv_total, head_depth
    )
    outgoing = jnp.broadcast_to(
        stacked, (2, ctx_size // split_count, split_count, quarter, kv_total, head_depth)
    )
    outgoing = outgoing.reshape(2, ctx_size, quarter, kv_total, head_depth)
    outgoing = jnp.where(wanted[None, :, None, None, None], outgoing, jnp.zeros((), outgoing.dtype))
    incoming = lax.all_to_all(outgoing, "ctx", split_axis=1, concat_axis=1, tiled=True)
    sources = (listed[:, None] * split_count + jnp.arange(split_count)[None, :]).reshape(-1)
    fetched = jnp.take(incoming, sources, axis=1)
    bit_total = split_count.bit_length() - 1
    for bit_index in range(bit_total):
        partner = from_partner(fetched, "ctx", bit_index)
        is_lower = my_member // 2**bit_index % 2 == 0
        fetched = jnp.where(
            is_lower,
            jnp.concatenate([fetched, partner], axis=2),
            jnp.concatenate([partner, fetched], axis=2),
        )
    fetched = fetched.reshape(2, slot_total * BLOCK, kv_total, head_depth)
    by_head = jnp.transpose(fetched, (0, 2, 1, 3))
    query_pos = my_index * token_count + jnp.arange(token_count)
    score_scale = 1.0 / math.sqrt(head_depth)
    grouped = queries.reshape(token_count, kv_total, groups, head_depth)
    offsets = jnp.arange(BLOCK)
    key_pos = (listed[:, None] * BLOCK + offsets[None, :]).reshape(-1)
    key_block = jnp.repeat(listed, BLOCK)
    key_valid = jnp.repeat(slot_valid, BLOCK)
    visibility = key_valid[None, :] & (
        (key_block[None, :] < my_block) | (key_pos[None, :] <= query_pos[:, None])
    )
    contract_last = (((1,), (1,)), ((), ()))
    head_outputs = []
    head_masses = []
    for kv_head in range(kv_total):
        key_head = by_head[0, kv_head]
        value_head = by_head[1, kv_head]
        for group_index in range(groups):
            raw_scores = (
                lax.dot_general(
                    grouped[:, kv_head, group_index],
                    key_head,
                    contract_last,
                    preferred_element_type=jnp.float32,
                )
                * score_scale
            )
            scores = jnp.where(visibility, raw_scores, -jnp.inf)
            highest = jnp.max(scores, axis=-1, keepdims=True)
            raised = jnp.exp(scores - highest)
            attention = raised / jnp.sum(raised, axis=-1, keepdims=True)
            head_outputs.append(
                jnp.dot(
                    attention.astype(jnp.bfloat16), value_head, preferred_element_type=jnp.float32
                )
            )
            head_masses.append(jnp.sum(attention, axis=0).reshape(slot_total, BLOCK))
    attn_out = jnp.stack(head_outputs, axis=1).astype(jnp.bfloat16)
    contrib = jnp.stack(head_masses, axis=1).reshape(
        slot_total, query_heads, split_count, token_count
    )
    contrib = jnp.transpose(contrib, (0, 2, 1, 3)).reshape(
        slot_total * split_count, query_heads, token_count
    )
    landing = jnp.zeros((ctx_size, query_heads, token_count), jnp.float32).at[sources].add(contrib)
    key_mass = lax.psum_scatter(landing, "ctx", scatter_dimension=0, tiled=True).reshape(
        query_heads, token_count
    )
    return (attn_out, key_mass)


def causal_kernel(
    n, q_hbm, k_hbm, v_hbm, out_ref, mass_ref,
    q_in, k_in, v_in, wide, q_all, k_all, v_all, scores, top, probs, mixed, mass, landed,
    in_sem, k_line, k_pair, k_recv, v_line, v_pair, v_recv, m_send, m_recv,
):
    me = lax.axis_index("ctx")
    level = me // 2
    side = me % 2
    levels = n // 2
    tokens, heads, depth = q_in.shape
    kv_total = heads // 8
    rows = tokens * 8
    partner = level * 2 + 1 - side
    log2_scale = math.log2(math.e) / math.sqrt(depth)

    copies_in = [
        pltpu.make_async_copy(src, dst, in_sem.at[i])
        for i, (src, dst) in enumerate(((k_hbm, k_in), (v_hbm, v_in), (q_hbm, q_in)))
    ]
    for copy in copies_in:
        copy.start()
    barrier = pltpu.get_barrier_semaphore()
    for hop in range(1, n):
        pl.semaphore_signal(
            barrier, inc=1, device_id={"ctx": lax.rem(me + hop, n)},
            device_id_type=pl.DeviceIdType.MESH,
        )

    def split_heads(source, target):
        wide[...] = source[...].astype(jnp.float32)
        for kv in range(kv_total):
            target[me, kv] = wide[pl.ds(kv, tokens, stride=kv_total), :].astype(jnp.bfloat16)

    def remote(ref, slot, send_sem, recv_sem, target, offset=0):
        return pltpu.make_async_remote_copy(
            src_ref=ref.at[slot], dst_ref=ref.at[slot],
            send_sem=send_sem.at[offset + slot], recv_sem=recv_sem.at[slot],
            device_id={"ctx": target}, device_id_type=pl.DeviceIdType.MESH,
        )

    def line_slot(back):
        return (level - back) * 2 + side

    def pair_slot(back):
        return (level - back) * 2 + 1 - side

    def has_line(back):
        return level >= back

    def has_pair(back):
        return (level >= back) & (side == 1) if back == 0 else level >= back

    def sends(ref, back, line_sem, pair_sem, recv_sem, act):
        slot = line_slot(back)

        for hop in (1, 2) if back % 2 == 0 else ():

            @pl.when((level >= back) & (level + hop < levels))
            def _():
                target = lax.rem(me + 2 * hop, n)
                act(remote(ref, slot, line_sem, recv_sem, target, (hop - 1) * n))

        gives = (level >= back) & (side == 0) if back == 0 else level >= back

        @pl.when(gives)
        def _():
            act(remote(ref, slot, pair_sem, recv_sem, partner))

    def send_k(back, act):
        sends(k_all, back, k_line, k_pair, k_recv, act)

    def send_v(back, act):
        sends(v_all, back, v_line, v_pair, v_recv, act)

    def start(copy):
        copy.start()

    def arrive(ref, slot, send_sem, recv_sem):
        remote(ref, slot, send_sem, recv_sem, partner).wait_recv()

    def forward_k(back):
        @pl.when(has_line(back))
        def _():
            arrive(k_all, line_slot(back), k_line, k_recv)

        send_k(back, start)

    def forward_v(back):
        @pl.when(has_line(back))
        def _():
            arrive(v_all, line_slot(back), v_line, v_recv)

        send_v(back, start)

    def score(slot, own):
        for kv in range(kv_total):
            raw = lax.dot_general(
                q_all[kv], k_all[slot, kv], (((1,), (1,)), ((), ())),
                preferred_element_type=jnp.float32,
            )
            if own:
                raw = raw.reshape(tokens, 8, tokens)
                token = lax.broadcasted_iota(jnp.int32, raw.shape, 0)
                key = lax.broadcasted_iota(jnp.int32, raw.shape, 2)
                raw = jnp.where(key <= token, raw, HIDDEN).reshape(rows, tokens)
                top[kv] = raw
            else:
                top[kv] = jnp.maximum(top[kv], raw)
            scores[slot, kv] = raw

    def score_line(back):
        @pl.when(has_line(back))
        def _():
            score(line_slot(back), False)

    def score_pair(back):
        @pl.when(has_pair(back))
        def _():
            slot = pair_slot(back)
            arrive(k_all, slot, k_pair, k_recv)
            score(slot, False)

    copies_in[0].wait()
    split_heads(k_in, k_all)
    pl.semaphore_wait(barrier, n - 1)
    send_k(0, start)
    copies_in[1].wait()
    split_heads(v_in, v_all)
    copies_in[2].wait()
    for kv in range(kv_total):
        q_part = q_in[...].astype(jnp.float32)[:, kv * 8 : kv * 8 + 8, :]
        q_all[kv] = q_part.reshape(rows, depth).astype(jnp.bfloat16)
    score(me, True)
    for slot in range(1, n):

        @pl.when(slot > me)
        def _():
            scores[slot] = jnp.full(scores.shape[1:], HIDDEN, jnp.float32)

    for back in range(1, levels):
        forward_k(back)
        if back == 1:
            send_v(0, start)
        score_line(back)
        score_pair(back - 1)
    score_pair(levels - 1)

    mass[...] = jnp.zeros_like(mass)
    part_rows = 128
    parts = rows // part_rows
    total = kv_total * parts

    def soften(index, carry):
        kv = index // parts
        at = pl.ds(pl.multiple_of((index % parts) * part_rows, part_rows), part_rows)
        highest = jnp.max(top[kv, at, :], axis=-1, keepdims=True) * log2_scale
        summed = jnp.zeros((part_rows, tokens), jnp.float32)
        for slot in range(n):
            raised = jnp.exp2(scores[slot, kv, at, :] * log2_scale - highest)
            scores[slot, kv, at, :] = raised
            summed = summed + raised
        inverse = 1.0 / jnp.sum(summed, axis=-1, keepdims=True)
        for slot in range(n):
            attention = scores[slot, kv, at, :] * inverse
            probs[slot, kv, at, :] = attention.astype(jnp.bfloat16)
            mass[slot, kv] += jnp.sum(attention.reshape(part_rows // 8, 8, tokens), axis=0)
        return carry

    for segment in range(SEGMENTS):
        if 1 + segment < levels:
            forward_v(1 + segment)
        lax.fori_loop(segment * total // SEGMENTS, (segment + 1) * total // SEGMENTS, soften, 0)

    def mass_copy(source, target):
        return pltpu.make_async_remote_copy(
            src_ref=mass.at[target], dst_ref=landed.at[source],
            send_sem=m_send.at[target], recv_sem=m_recv.at[source],
            device_id={"ctx": target}, device_id_type=pl.DeviceIdType.MESH,
        )

    for slot in range(n - 1):

        @pl.when(slot < me)
        def _():
            mass_copy(me, slot).start()

    def mix(slot, first):
        for kv in range(kv_total):
            piece = jnp.dot(probs[slot, kv], v_all[slot, kv], preferred_element_type=jnp.float32)
            mixed[kv] = piece if first else mixed[kv] + piece

    def mix_line(back):
        @pl.when(has_line(back))
        def _():
            mix(line_slot(back), False)

    def mix_pair(back):
        @pl.when(has_pair(back))
        def _():
            slot = pair_slot(back)
            arrive(v_all, slot, v_pair, v_recv)
            mix(slot, False)

    mix(me, True)
    for back in range(1, levels):
        mix_line(back)
        mix_pair(back - 1)
    mix_pair(levels - 1)
    out_ref[...] = jnp.concatenate(
        [mixed[kv].reshape(tokens, 8, depth) for kv in range(kv_total)], axis=1
    ).astype(out_ref.dtype)

    mass_ref[...] = jnp.concatenate([mass[me, kv] for kv in range(kv_total)], axis=0)
    for slot in range(1, n):

        @pl.when(slot > me)
        def _():
            mass_copy(slot, me * 0 + partner).wait_recv()
            mass_ref[...] += jnp.concatenate([landed[slot, kv] for kv in range(kv_total)], axis=0)

    def wait_send(copy):
        copy.wait_send()

    for back in range(levels):
        send_k(back, wait_send)
        send_v(back, wait_send)
    for slot in range(n - 1):

        @pl.when(slot < me)
        def _():
            mass_copy(me, slot).wait_send()


def causal_step(n, queries, key_states, value_states):
    tokens, heads, depth = queries.shape
    kv_total = key_states.shape[1]
    rows = tokens * 8
    f32, bf16 = jnp.float32, jnp.bfloat16
    dma = pltpu.SemaphoreType.DMA
    return pl.pallas_call(
        functools.partial(causal_kernel, n),
        out_shape=(
            jax.ShapeDtypeStruct((tokens, heads, depth), bf16),
            jax.ShapeDtypeStruct((heads, tokens), f32),
        ),
        in_specs=[pl.BlockSpec(memory_space=pltpu.HBM)] * 3,
        out_specs=[pl.BlockSpec(memory_space=pltpu.VMEM)] * 2,
        scratch_shapes=[
            pltpu.VMEM((tokens, heads, depth), bf16),
            pltpu.VMEM((tokens * kv_total, depth), bf16),
            pltpu.VMEM((tokens * kv_total, depth), bf16),
            pltpu.VMEM((tokens * kv_total, depth), f32),
            pltpu.VMEM((kv_total, rows, depth), bf16),
            pltpu.VMEM((n, kv_total, tokens, depth), bf16),
            pltpu.VMEM((n, kv_total, tokens, depth), bf16),
            pltpu.VMEM((n, kv_total, rows, tokens), f32),
            pltpu.VMEM((kv_total, rows, tokens), f32),
            pltpu.VMEM((n, kv_total, rows, tokens), bf16),
            pltpu.VMEM((kv_total, rows, depth), f32),
            pltpu.VMEM((n, kv_total, 8, tokens), f32),
            pltpu.VMEM((n, kv_total, 8, tokens), f32),
            dma((3,)), dma((2 * n,)), dma((n,)), dma((n,)), dma((2 * n,)), dma((n,)), dma((n,)),
            dma((n,)), dma((n,)),
        ],
        compiler_params=pltpu.CompilerParams(
            collective_id=0, has_side_effects=True, vmem_limit_bytes=62 * 1024 * 1024
        ),
    )(
        queries,
        key_states.reshape(tokens * kv_total, depth),
        value_states.reshape(tokens * kv_total, depth),
    )


def solution(mesh):
    in_specs = (P("ctx", "head", None), P("ctx", "head", None), P("ctx", "head", None), P(), P())
    out_specs = (P("ctx", "head", None), P("head", "ctx"))

    def step(queries, key_states, value_states, chosen, valid_count):
        if chosen.shape[0] <= 2 and mesh.shape["ctx"] % 2 == 0:
            return causal_step(mesh.shape["ctx"], queries, key_states, value_states)
        return on_device(queries, key_states, value_states, chosen, valid_count)

    return jax.shard_map(step, mesh=mesh, in_specs=in_specs, out_specs=out_specs, check_vma=False)
```

```python
import functools
import math

import jax
import jax.numpy as jnp
from jax import lax
from jax.experimental import pallas as pl
from jax.experimental.pallas import tpu as pltpu
from jax.sharding import PartitionSpec as P

BLOCK = 512
HIDDEN = -1e30
SEGMENTS = 4


def from_partner(value, axis, bit):
    mask = 2**bit
    pairs = [(source, source ^ mask) for source in range(lax.axis_size(axis))]
    return lax.ppermute(value, axis, pairs)


def on_device(queries, key_states, value_states, chosen, valid_count):
    ctx_size = lax.axis_size("ctx")
    my_index = lax.axis_index("ctx")
    token_count = queries.shape[0]
    query_heads = queries.shape[1]
    head_depth = queries.shape[2]
    kv_total = key_states.shape[1]
    groups = query_heads // kv_total
    slot_total = chosen.shape[1]
    split_count = BLOCK // token_count
    quarter = token_count // split_count
    my_block = my_index // split_count
    my_member = my_index % split_count
    listed = chosen[my_block]
    slot_ids = jnp.arange(slot_total)
    slot_valid = slot_ids < valid_count[my_block]
    owners = jnp.arange(ctx_size) // split_count
    wanted = jnp.any(
        (slot_ids[None, :] < valid_count[owners][:, None]) & (chosen[owners] == my_block), axis=1
    )
    stacked = jnp.stack([key_states, value_states]).reshape(
        2, 1, split_count, quarter, kv_total, head_depth
    )
    outgoing = jnp.broadcast_to(
        stacked, (2, ctx_size // split_count, split_count, quarter, kv_total, head_depth)
    )
    outgoing = outgoing.reshape(2, ctx_size, quarter, kv_total, head_depth)
    outgoing = jnp.where(wanted[None, :, None, None, None], outgoing, jnp.zeros((), outgoing.dtype))
    incoming = lax.all_to_all(outgoing, "ctx", split_axis=1, concat_axis=1, tiled=True)
    sources = (listed[:, None] * split_count + jnp.arange(split_count)[None, :]).reshape(-1)
    fetched = jnp.take(incoming, sources, axis=1)
    bit_total = split_count.bit_length() - 1
    for bit_index in range(bit_total):
        partner = from_partner(fetched, "ctx", bit_index)
        is_lower = my_member // 2**bit_index % 2 == 0
        fetched = jnp.where(
            is_lower,
            jnp.concatenate([fetched, partner], axis=2),
            jnp.concatenate([partner, fetched], axis=2),
        )
    fetched = fetched.reshape(2, slot_total * BLOCK, kv_total, head_depth)
    by_head = jnp.transpose(fetched, (0, 2, 1, 3))
    query_pos = my_index * token_count + jnp.arange(token_count)
    score_scale = 1.0 / math.sqrt(head_depth)
    grouped = queries.reshape(token_count, kv_total, groups, head_depth)
    offsets = jnp.arange(BLOCK)
    key_pos = (listed[:, None] * BLOCK + offsets[None, :]).reshape(-1)
    key_block = jnp.repeat(listed, BLOCK)
    key_valid = jnp.repeat(slot_valid, BLOCK)
    visibility = key_valid[None, :] & (
        (key_block[None, :] < my_block) | (key_pos[None, :] <= query_pos[:, None])
    )
    contract_last = (((1,), (1,)), ((), ()))
    head_outputs = []
    head_masses = []
    for kv_head in range(kv_total):
        key_head = by_head[0, kv_head]
        value_head = by_head[1, kv_head]
        for group_index in range(groups):
            raw_scores = (
                lax.dot_general(
                    grouped[:, kv_head, group_index],
                    key_head,
                    contract_last,
                    preferred_element_type=jnp.float32,
                )
                * score_scale
            )
            scores = jnp.where(visibility, raw_scores, -jnp.inf)
            highest = jnp.max(scores, axis=-1, keepdims=True)
            raised = jnp.exp(scores - highest)
            attention = raised / jnp.sum(raised, axis=-1, keepdims=True)
            head_outputs.append(
                jnp.dot(
                    attention.astype(jnp.bfloat16), value_head, preferred_element_type=jnp.float32
                )
            )
            head_masses.append(jnp.sum(attention, axis=0).reshape(slot_total, BLOCK))
    attn_out = jnp.stack(head_outputs, axis=1).astype(jnp.bfloat16)
    contrib = jnp.stack(head_masses, axis=1).reshape(
        slot_total, query_heads, split_count, token_count
    )
    contrib = jnp.transpose(contrib, (0, 2, 1, 3)).reshape(
        slot_total * split_count, query_heads, token_count
    )
    landing = jnp.zeros((ctx_size, query_heads, token_count), jnp.float32).at[sources].add(contrib)
    key_mass = lax.psum_scatter(landing, "ctx", scatter_dimension=0, tiled=True).reshape(
        query_heads, token_count
    )
    return (attn_out, key_mass)


def causal_kernel(
    n, q_hbm, k_hbm, v_hbm, out_ref, mass_ref,
    q_in, k_in, v_in, wide, q_all, k_all, v_all, scores, top, probs, mixed, mass, landed,
    in_sem, k_line, k_pair, k_recv, v_line, v_pair, v_recv, m_send, m_recv,
):
    me = lax.axis_index("ctx")
    level = me // 2
    side = me % 2
    levels = n // 2
    tokens, heads, depth = q_in.shape
    kv_total = heads // 8
    rows = tokens * 8
    partner = level * 2 + 1 - side
    log2_scale = math.log2(math.e) / math.sqrt(depth)

    copies_in = [
        pltpu.make_async_copy(src, dst, in_sem.at[i])
        for i, (src, dst) in enumerate(((k_hbm, k_in), (v_hbm, v_in), (q_hbm, q_in)))
    ]
    for copy in copies_in:
        copy.start()
    barrier = pltpu.get_barrier_semaphore()
    for hop in range(1, n):
        pl.semaphore_signal(
            barrier, inc=1, device_id={"ctx": lax.rem(me + hop, n)},
            device_id_type=pl.DeviceIdType.MESH,
        )

    def split_heads(source, target):
        wide[...] = source[...].astype(jnp.float32)
        for kv in range(kv_total):
            target[me, kv] = wide[pl.ds(kv, tokens, stride=kv_total), :].astype(jnp.bfloat16)

    def remote(ref, slot, kv, send_sem, recv_sem, target, hop=0):
        return pltpu.make_async_remote_copy(
            src_ref=ref.at[slot, kv], dst_ref=ref.at[slot, kv],
            send_sem=send_sem.at[hop, slot, kv], recv_sem=recv_sem.at[slot, kv],
            device_id={"ctx": target}, device_id_type=pl.DeviceIdType.MESH,
        )

    def line_slot(back):
        return (level - back) * 2 + side

    def pair_slot(back):
        return (level - back) * 2 + 1 - side

    def has_line(back):
        return level >= back

    def has_pair(back):
        return (level >= back) & (side == 1) if back == 0 else level >= back

    def sends(ref, back, kv, line_sem, pair_sem, recv_sem, act):
        slot = line_slot(back)

        for hop in (1, 2) if back % 2 == 0 else ():

            @pl.when((level >= back) & (level + hop < levels))
            def _():
                target = lax.rem(me + 2 * hop, n)
                act(remote(ref, slot, kv, line_sem, recv_sem, target, hop - 1))

        gives = (level >= back) & (side == 0) if back == 0 else level >= back

        @pl.when(gives)
        def _():
            act(remote(ref, slot, kv, pair_sem, recv_sem, partner))

    def send_k(back, act):
        for kv in range(kv_total):
            sends(k_all, back, kv, k_line, k_pair, k_recv, act)

    def send_v(back, act):
        for kv in range(kv_total):
            sends(v_all, back, kv, v_line, v_pair, v_recv, act)

    def start(copy):
        copy.start()

    def arrive_part(ref, slot, kv, send_sem, recv_sem):
        remote(ref, slot, kv, send_sem, recv_sem, partner).wait_recv()

    def arrive(ref, slot, send_sem, recv_sem):
        for kv in range(kv_total):
            arrive_part(ref, slot, kv, send_sem, recv_sem)

    def forward_k(back):
        for kv in range(kv_total):

            @pl.when(has_line(back))
            def _():
                arrive_part(k_all, line_slot(back), kv, k_line, k_recv)

            sends(k_all, back, kv, k_line, k_pair, k_recv, start)

    def forward_v(back):
        for kv in range(kv_total):

            @pl.when(has_line(back))
            def _():
                arrive_part(v_all, line_slot(back), kv, v_line, v_recv)

            sends(v_all, back, kv, v_line, v_pair, v_recv, start)

    def score(slot, own):
        for kv in range(kv_total):
            raw = lax.dot_general(
                q_all[kv], k_all[slot, kv], (((1,), (1,)), ((), ())),
                preferred_element_type=jnp.float32,
            )
            raw = raw * log2_scale
            if own:
                raw = raw.reshape(tokens, 8, tokens)
                token = lax.broadcasted_iota(jnp.int32, raw.shape, 0)
                key = lax.broadcasted_iota(jnp.int32, raw.shape, 2)
                raw = jnp.where(key <= token, raw, HIDDEN).reshape(rows, tokens)
                top[kv] = raw
            else:
                top[kv] = jnp.maximum(top[kv], raw)
            scores[slot, kv] = raw

    def score_line(back):
        @pl.when(has_line(back))
        def _():
            score(line_slot(back), False)

    def score_pair(back):
        @pl.when(has_pair(back))
        def _():
            slot = pair_slot(back)
            arrive(k_all, slot, k_pair, k_recv)
            score(slot, False)

    copies_in[0].wait()
    split_heads(k_in, k_all)
    pl.semaphore_wait(barrier, n - 1)
    send_k(0, start)
    copies_in[1].wait()
    split_heads(v_in, v_all)
    copies_in[2].wait()
    for kv in range(kv_total):
        q_part = q_in[...].astype(jnp.float32)[:, kv * 8 : kv * 8 + 8, :]
        q_all[kv] = q_part.reshape(rows, depth).astype(jnp.bfloat16)
    score(me, True)
    for slot in range(1, n):

        @pl.when(slot > me)
        def _():
            scores[slot] = jnp.full(scores.shape[1:], HIDDEN, jnp.float32)

    for back in range(1, levels):
        forward_k(back)
        if back == 1:
            send_v(0, start)
        score_line(back)
        if back >= 2:
            score_pair(back - 2)
    if levels > 1:
        forward_v(1)
        score_pair(levels - 2)
    score_pair(levels - 1)

    mass[...] = jnp.zeros_like(mass)
    part_rows = 512
    parts = rows // part_rows
    total = kv_total * parts

    def soften(index, carry):
        kv = index // parts
        at = pl.ds(pl.multiple_of((index % parts) * part_rows, part_rows), part_rows)
        highest = jnp.max(top[kv, at, :], axis=-1, keepdims=True)
        summed = jnp.zeros((part_rows, tokens), jnp.float32)
        for slot in range(n):
            raised = jnp.exp2(scores[slot, kv, at, :] - highest)
            scores[slot, kv, at, :] = raised
            summed = summed + raised
        inverse = 1.0 / jnp.sum(summed, axis=-1, keepdims=True)
        for slot in range(n):
            attention = scores[slot, kv, at, :] * inverse
            probs[slot, kv, at, :] = attention.astype(jnp.bfloat16)
            mass[slot, kv] += jnp.sum(attention.reshape(part_rows // 8, 8, tokens), axis=0)
        return carry

    for segment in range(SEGMENTS):
        if 2 + segment < levels:
            forward_v(2 + segment)
        lax.fori_loop(segment * total // SEGMENTS, (segment + 1) * total // SEGMENTS, soften, 0)

    def mass_copy(source, target):
        return pltpu.make_async_remote_copy(
            src_ref=mass.at[target], dst_ref=landed.at[source],
            send_sem=m_send.at[target], recv_sem=m_recv.at[source],
            device_id={"ctx": target}, device_id_type=pl.DeviceIdType.MESH,
        )

    for slot in range(n - 1):

        @pl.when(slot < me)
        def _():
            mass_copy(me, slot).start()

    def mix(slot, first):
        for kv in range(kv_total):
            piece = jnp.dot(probs[slot, kv], v_all[slot, kv], preferred_element_type=jnp.float32)
            mixed[kv] = piece if first else mixed[kv] + piece

    def mix_line(back):
        @pl.when(has_line(back))
        def _():
            mix(line_slot(back), False)

    def mix_pair(back):
        @pl.when(has_pair(back))
        def _():
            slot = pair_slot(back)
            arrive(v_all, slot, v_pair, v_recv)
            mix(slot, False)

    mix(me, True)
    for back in range(1, levels):
        mix_line(back)
        mix_pair(back - 1)
    mix_pair(levels - 1)
    out_ref[...] = jnp.concatenate(
        [mixed[kv].reshape(tokens, 8, depth) for kv in range(kv_total)], axis=1
    ).astype(out_ref.dtype)

    mass_ref[...] = jnp.concatenate([mass[me, kv] for kv in range(kv_total)], axis=0)
    for slot in range(1, n):

        @pl.when(slot > me)
        def _():
            mass_copy(slot, me * 0 + partner).wait_recv()
            mass_ref[...] += jnp.concatenate([landed[slot, kv] for kv in range(kv_total)], axis=0)

    def wait_send(copy):
        copy.wait_send()

    for back in range(levels):
        send_k(back, wait_send)
        send_v(back, wait_send)
    for slot in range(n - 1):

        @pl.when(slot < me)
        def _():
            mass_copy(me, slot).wait_send()


def causal_step(n, queries, key_states, value_states):
    tokens, heads, depth = queries.shape
    kv_total = key_states.shape[1]
    rows = tokens * 8
    f32, bf16 = jnp.float32, jnp.bfloat16
    dma = pltpu.SemaphoreType.DMA
    return pl.pallas_call(
        functools.partial(causal_kernel, n),
        out_shape=(
            jax.ShapeDtypeStruct((tokens, heads, depth), bf16),
            jax.ShapeDtypeStruct((heads, tokens), f32),
        ),
        in_specs=[pl.BlockSpec(memory_space=pltpu.HBM)] * 3,
        out_specs=[pl.BlockSpec(memory_space=pltpu.VMEM)] * 2,
        scratch_shapes=[
            pltpu.VMEM((tokens, heads, depth), bf16),
            pltpu.VMEM((tokens * kv_total, depth), bf16),
            pltpu.VMEM((tokens * kv_total, depth), bf16),
            pltpu.VMEM((tokens * kv_total, depth), f32),
            pltpu.VMEM((kv_total, rows, depth), bf16),
            pltpu.VMEM((n, kv_total, tokens, depth), bf16),
            pltpu.VMEM((n, kv_total, tokens, depth), bf16),
            pltpu.VMEM((n, kv_total, rows, tokens), f32),
            pltpu.VMEM((kv_total, rows, tokens), f32),
            pltpu.VMEM((n, kv_total, rows, tokens), bf16),
            pltpu.VMEM((kv_total, rows, depth), f32),
            pltpu.VMEM((n, kv_total, 8, tokens), f32),
            pltpu.VMEM((n, kv_total, 8, tokens), f32),
            dma((3,)), dma((2, n, kv_total)), dma((1, n, kv_total)), dma((n, kv_total)),
            dma((2, n, kv_total)), dma((1, n, kv_total)), dma((n, kv_total)),
            dma((n,)), dma((n,)),
        ],
        compiler_params=pltpu.CompilerParams(
            collective_id=0, has_side_effects=True, vmem_limit_bytes=62 * 1024 * 1024
        ),
    )(
        queries,
        key_states.reshape(tokens * kv_total, depth),
        value_states.reshape(tokens * kv_total, depth),
    )


def solution(mesh):
    in_specs = (P("ctx", "head", None), P("ctx", "head", None), P("ctx", "head", None), P(), P())
    out_specs = (P("ctx", "head", None), P("head", "ctx"))

    def step(queries, key_states, value_states, chosen, valid_count):
        if chosen.shape[0] <= 2 and mesh.shape["ctx"] % 2 == 0:
            return causal_step(mesh.shape["ctx"], queries, key_states, value_states)
        return on_device(queries, key_states, value_states, chosen, valid_count)

    return jax.shard_map(step, mesh=mesh, in_specs=in_specs, out_specs=out_specs, check_vma=False)
```

```python
import functools
import math

import jax
import jax.numpy as jnp
from jax import lax
from jax.experimental import pallas as pl
from jax.experimental.pallas import tpu as pltpu
from jax.sharding import PartitionSpec as P

BLOCK = 512
HIDDEN = -1e30
SEGMENTS = 2


def from_partner(value, axis, bit):
    mask = 2**bit
    pairs = [(source, source ^ mask) for source in range(lax.axis_size(axis))]
    return lax.ppermute(value, axis, pairs)


def on_device(queries, key_states, value_states, chosen, valid_count):
    ctx_size = lax.axis_size("ctx")
    my_index = lax.axis_index("ctx")
    token_count = queries.shape[0]
    query_heads = queries.shape[1]
    head_depth = queries.shape[2]
    kv_total = key_states.shape[1]
    groups = query_heads // kv_total
    slot_total = chosen.shape[1]
    split_count = BLOCK // token_count
    quarter = token_count // split_count
    my_block = my_index // split_count
    my_member = my_index % split_count
    listed = chosen[my_block]
    slot_ids = jnp.arange(slot_total)
    slot_valid = slot_ids < valid_count[my_block]
    owners = jnp.arange(ctx_size) // split_count
    wanted = jnp.any(
        (slot_ids[None, :] < valid_count[owners][:, None]) & (chosen[owners] == my_block), axis=1
    )
    stacked = jnp.stack([key_states, value_states]).reshape(
        2, 1, split_count, quarter, kv_total, head_depth
    )
    outgoing = jnp.broadcast_to(
        stacked, (2, ctx_size // split_count, split_count, quarter, kv_total, head_depth)
    )
    outgoing = outgoing.reshape(2, ctx_size, quarter, kv_total, head_depth)
    outgoing = jnp.where(wanted[None, :, None, None, None], outgoing, jnp.zeros((), outgoing.dtype))
    incoming = lax.all_to_all(outgoing, "ctx", split_axis=1, concat_axis=1, tiled=True)
    sources = (listed[:, None] * split_count + jnp.arange(split_count)[None, :]).reshape(-1)
    fetched = jnp.take(incoming, sources, axis=1)
    bit_total = split_count.bit_length() - 1
    for bit_index in range(bit_total):
        partner = from_partner(fetched, "ctx", bit_index)
        is_lower = my_member // 2**bit_index % 2 == 0
        fetched = jnp.where(
            is_lower,
            jnp.concatenate([fetched, partner], axis=2),
            jnp.concatenate([partner, fetched], axis=2),
        )
    fetched = fetched.reshape(2, slot_total * BLOCK, kv_total, head_depth)
    by_head = jnp.transpose(fetched, (0, 2, 1, 3))
    query_pos = my_index * token_count + jnp.arange(token_count)
    score_scale = 1.0 / math.sqrt(head_depth)
    grouped = queries.reshape(token_count, kv_total, groups, head_depth)
    offsets = jnp.arange(BLOCK)
    key_pos = (listed[:, None] * BLOCK + offsets[None, :]).reshape(-1)
    key_block = jnp.repeat(listed, BLOCK)
    key_valid = jnp.repeat(slot_valid, BLOCK)
    visibility = key_valid[None, :] & (
        (key_block[None, :] < my_block) | (key_pos[None, :] <= query_pos[:, None])
    )
    contract_last = (((1,), (1,)), ((), ()))
    head_outputs = []
    head_masses = []
    for kv_head in range(kv_total):
        key_head = by_head[0, kv_head]
        value_head = by_head[1, kv_head]
        for group_index in range(groups):
            raw_scores = (
                lax.dot_general(
                    grouped[:, kv_head, group_index],
                    key_head,
                    contract_last,
                    preferred_element_type=jnp.float32,
                )
                * score_scale
            )
            scores = jnp.where(visibility, raw_scores, -jnp.inf)
            highest = jnp.max(scores, axis=-1, keepdims=True)
            raised = jnp.exp(scores - highest)
            attention = raised / jnp.sum(raised, axis=-1, keepdims=True)
            head_outputs.append(
                jnp.dot(
                    attention.astype(jnp.bfloat16), value_head, preferred_element_type=jnp.float32
                )
            )
            head_masses.append(jnp.sum(attention, axis=0).reshape(slot_total, BLOCK))
    attn_out = jnp.stack(head_outputs, axis=1).astype(jnp.bfloat16)
    contrib = jnp.stack(head_masses, axis=1).reshape(
        slot_total, query_heads, split_count, token_count
    )
    contrib = jnp.transpose(contrib, (0, 2, 1, 3)).reshape(
        slot_total * split_count, query_heads, token_count
    )
    landing = jnp.zeros((ctx_size, query_heads, token_count), jnp.float32).at[sources].add(contrib)
    key_mass = lax.psum_scatter(landing, "ctx", scatter_dimension=0, tiled=True).reshape(
        query_heads, token_count
    )
    return (attn_out, key_mass)


def causal_kernel(
    n, q_hbm, k_hbm, v_hbm, out_ref, mass_ref,
    q_in, k_in, v_in, wide, q_all, k_all, v_all, scores, top, probs, mixed, mass, landed,
    in_sem, k_line, k_pair, k_recv, v_line, v_pair, v_recv, m_send, m_recv,
):
    me = lax.axis_index("ctx")
    level = me // 2
    side = me % 2
    levels = n // 2
    tokens, heads, depth = q_in.shape
    kv_total = heads // 8
    rows = tokens * 8
    partner = level * 2 + 1 - side
    log2_scale = math.log2(math.e) / math.sqrt(depth)

    copies_in = [
        pltpu.make_async_copy(src, dst, in_sem.at[i])
        for i, (src, dst) in enumerate(((k_hbm, k_in), (v_hbm, v_in), (q_hbm, q_in)))
    ]
    for copy in copies_in:
        copy.start()
    barrier = pltpu.get_barrier_semaphore()
    for hop in range(1, n):
        pl.semaphore_signal(
            barrier, inc=1, device_id={"ctx": lax.rem(me + hop, n)},
            device_id_type=pl.DeviceIdType.MESH,
        )

    def split_heads(source, target):
        wide[...] = source[...].astype(jnp.float32)
        for kv in range(kv_total):
            target[me, kv] = wide[pl.ds(kv, tokens, stride=kv_total), :].astype(jnp.bfloat16)

    def remote(ref, slot, kv, send_sem, recv_sem, target, hop=0):
        return pltpu.make_async_remote_copy(
            src_ref=ref.at[slot, kv], dst_ref=ref.at[slot, kv],
            send_sem=send_sem.at[hop, slot, kv], recv_sem=recv_sem.at[slot, kv],
            device_id={"ctx": target}, device_id_type=pl.DeviceIdType.MESH,
        )

    def line_slot(back):
        return (level - back) * 2 + side

    def pair_slot(back):
        return (level - back) * 2 + 1 - side

    def has_line(back):
        return level >= back

    def has_pair(back):
        return (level >= back) & (side == 1) if back == 0 else level >= back

    def sends(ref, back, kv, line_sem, pair_sem, recv_sem, act):
        slot = line_slot(back)

        for hop in (1, 2) if back % 2 == 0 else ():

            @pl.when((level >= back) & (level + hop < levels))
            def _():
                target = lax.rem(me + 2 * hop, n)
                act(remote(ref, slot, kv, line_sem, recv_sem, target, hop - 1))

        gives = (level >= back) & (side == 0) if back == 0 else level >= back

        @pl.when(gives)
        def _():
            act(remote(ref, slot, kv, pair_sem, recv_sem, partner))

    def send_k(back, act):
        for kv in range(kv_total):
            sends(k_all, back, kv, k_line, k_pair, k_recv, act)

    def send_v(back, act):
        for kv in range(kv_total):
            sends(v_all, back, kv, v_line, v_pair, v_recv, act)

    def start(copy):
        copy.start()

    def arrive_part(ref, slot, kv, send_sem, recv_sem):
        remote(ref, slot, kv, send_sem, recv_sem, partner).wait_recv()

    def arrive(ref, slot, send_sem, recv_sem):
        for kv in range(kv_total):
            arrive_part(ref, slot, kv, send_sem, recv_sem)

    def forward_k(back):
        for kv in range(kv_total):

            @pl.when(has_line(back))
            def _():
                arrive_part(k_all, line_slot(back), kv, k_line, k_recv)

            sends(k_all, back, kv, k_line, k_pair, k_recv, start)

    def forward_v(back):
        for kv in range(kv_total):

            @pl.when(has_line(back))
            def _():
                arrive_part(v_all, line_slot(back), kv, v_line, v_recv)

            sends(v_all, back, kv, v_line, v_pair, v_recv, start)

    def score(slot, own):
        for kv in range(kv_total):
            raw = lax.dot_general(
                q_all[kv], k_all[slot, kv], (((1,), (1,)), ((), ())),
                preferred_element_type=jnp.float32,
            )
            raw = raw * log2_scale
            if own:
                raw = raw.reshape(tokens, 8, tokens)
                token = lax.broadcasted_iota(jnp.int32, raw.shape, 0)
                key = lax.broadcasted_iota(jnp.int32, raw.shape, 2)
                raw = jnp.where(key <= token, raw, HIDDEN).reshape(rows, tokens)
                top[kv] = raw
            else:
                top[kv] = jnp.maximum(top[kv], raw)
            scores[slot, kv] = raw

    def score_line(back):
        @pl.when(has_line(back))
        def _():
            score(line_slot(back), False)

    def score_pair(back):
        @pl.when(has_pair(back))
        def _():
            slot = pair_slot(back)
            arrive(k_all, slot, k_pair, k_recv)
            score(slot, False)

    copies_in[0].wait()
    split_heads(k_in, k_all)
    pl.semaphore_wait(barrier, n - 1)
    send_k(0, start)
    copies_in[1].wait()
    split_heads(v_in, v_all)
    copies_in[2].wait()
    for kv in range(kv_total):
        q_part = q_in[...].astype(jnp.float32)[:, kv * 8 : kv * 8 + 8, :]
        q_all[kv] = q_part.reshape(rows, depth).astype(jnp.bfloat16)
    score(me, True)
    for slot in range(1, n):

        @pl.when(slot > me)
        def _():
            scores[slot] = jnp.full(scores.shape[1:], HIDDEN, jnp.float32)

    for back in range(1, levels):
        forward_k(back)
        if back == 1:
            send_v(0, start)
        score_line(back)
        if back >= 2:
            score_pair(back - 2)
    if levels > 1:
        forward_v(1)
        score_pair(levels - 2)
    score_pair(levels - 1)

    mass[...] = jnp.zeros_like(mass)
    part_rows = 1024
    parts = rows // part_rows
    total = kv_total * parts

    def soften(index, carry):
        kv = index // parts
        at = pl.ds(pl.multiple_of((index % parts) * part_rows, part_rows), part_rows)
        highest = jnp.max(top[kv, at, :], axis=-1, keepdims=True)
        summed = jnp.zeros((part_rows, tokens), jnp.float32)
        for slot in range(n):
            raised = jnp.exp2(scores[slot, kv, at, :] - highest)
            scores[slot, kv, at, :] = raised
            summed = summed + raised
        inverse = 1.0 / jnp.sum(summed, axis=-1, keepdims=True)
        for slot in range(n):
            attention = scores[slot, kv, at, :] * inverse
            probs[slot, kv, at, :] = attention.astype(jnp.bfloat16)
            mass[slot, kv] += jnp.sum(attention.reshape(part_rows // 8, 8, tokens), axis=0)
        return carry

    for segment in range(SEGMENTS):
        for back in range(2 + segment, levels, SEGMENTS):
            forward_v(back)
        lax.fori_loop(segment * total // SEGMENTS, (segment + 1) * total // SEGMENTS, soften, 0)

    def mass_copy(source, target):
        return pltpu.make_async_remote_copy(
            src_ref=mass.at[target], dst_ref=landed.at[source],
            send_sem=m_send.at[target], recv_sem=m_recv.at[source],
            device_id={"ctx": target}, device_id_type=pl.DeviceIdType.MESH,
        )

    for slot in range(n - 1):

        @pl.when(slot < me)
        def _():
            mass_copy(me, slot).start()

    def mix(slot, first):
        for kv in range(kv_total):
            piece = jnp.dot(probs[slot, kv], v_all[slot, kv], preferred_element_type=jnp.float32)
            mixed[kv] = piece if first else mixed[kv] + piece

    def mix_line(back):
        @pl.when(has_line(back))
        def _():
            mix(line_slot(back), False)

    def mix_pair(back):
        @pl.when(has_pair(back))
        def _():
            slot = pair_slot(back)
            arrive(v_all, slot, v_pair, v_recv)
            mix(slot, False)

    mix(me, True)
    for back in range(1, levels):
        mix_line(back)
        mix_pair(back - 1)
    mix_pair(levels - 1)
    out_ref[...] = jnp.concatenate(
        [mixed[kv].reshape(tokens, 8, depth) for kv in range(kv_total)], axis=1
    ).astype(out_ref.dtype)

    mass_ref[...] = jnp.concatenate([mass[me, kv] for kv in range(kv_total)], axis=0)
    for slot in range(1, n):

        @pl.when(slot > me)
        def _():
            mass_copy(slot, me * 0 + partner).wait_recv()
            mass_ref[...] += jnp.concatenate([landed[slot, kv] for kv in range(kv_total)], axis=0)

    def wait_send(copy):
        copy.wait_send()

    for back in range(levels):
        send_k(back, wait_send)
        send_v(back, wait_send)
    for slot in range(n - 1):

        @pl.when(slot < me)
        def _():
            mass_copy(me, slot).wait_send()


def causal_step(n, queries, key_states, value_states):
    tokens, heads, depth = queries.shape
    kv_total = key_states.shape[1]
    rows = tokens * 8
    f32, bf16 = jnp.float32, jnp.bfloat16
    dma = pltpu.SemaphoreType.DMA
    return pl.pallas_call(
        functools.partial(causal_kernel, n),
        out_shape=(
            jax.ShapeDtypeStruct((tokens, heads, depth), bf16),
            jax.ShapeDtypeStruct((heads, tokens), f32),
        ),
        in_specs=[pl.BlockSpec(memory_space=pltpu.HBM)] * 3,
        out_specs=[pl.BlockSpec(memory_space=pltpu.VMEM)] * 2,
        scratch_shapes=[
            pltpu.VMEM((tokens, heads, depth), bf16),
            pltpu.VMEM((tokens * kv_total, depth), bf16),
            pltpu.VMEM((tokens * kv_total, depth), bf16),
            pltpu.VMEM((tokens * kv_total, depth), f32),
            pltpu.VMEM((kv_total, rows, depth), bf16),
            pltpu.VMEM((n, kv_total, tokens, depth), bf16),
            pltpu.VMEM((n, kv_total, tokens, depth), bf16),
            pltpu.VMEM((n, kv_total, rows, tokens), f32),
            pltpu.VMEM((kv_total, rows, tokens), f32),
            pltpu.VMEM((n, kv_total, rows, tokens), bf16),
            pltpu.VMEM((kv_total, rows, depth), f32),
            pltpu.VMEM((n, kv_total, 8, tokens), f32),
            pltpu.VMEM((n, kv_total, 8, tokens), f32),
            dma((3,)), dma((2, n, kv_total)), dma((1, n, kv_total)), dma((n, kv_total)),
            dma((2, n, kv_total)), dma((1, n, kv_total)), dma((n, kv_total)),
            dma((n,)), dma((n,)),
        ],
        compiler_params=pltpu.CompilerParams(
            collective_id=0, has_side_effects=True, vmem_limit_bytes=62 * 1024 * 1024
        ),
    )(
        queries,
        key_states.reshape(tokens * kv_total, depth),
        value_states.reshape(tokens * kv_total, depth),
    )


def solution(mesh):
    in_specs = (P("ctx", "head", None), P("ctx", "head", None), P("ctx", "head", None), P(), P())
    out_specs = (P("ctx", "head", None), P("head", "ctx"))

    def step(queries, key_states, value_states, chosen, valid_count):
        if chosen.shape[0] <= 2 and mesh.shape["ctx"] % 2 == 0:
            return causal_step(mesh.shape["ctx"], queries, key_states, value_states)
        return on_device(queries, key_states, value_states, chosen, valid_count)

    return jax.shard_map(step, mesh=mesh, in_specs=in_specs, out_specs=out_specs, check_vma=False)
```
